32 devices in a mesh: clip: 4 (over z), row: 4 (over y, x), col: 2 (over core).
Axes of the slice: x: 2, y: 2, z: 4, core: 2. Of those that a mesh axis runs over, the one named last changes fastest.
Arguments:
- current: bfloat16 [4, 64, 32, 256], P('clip', 'row', 'col'), may hold values from -6 to 6
- bank: bfloat16 [4, 8, 64, 32, 256], P('clip', None, 'row', 'col'), may hold values from -6 to 6
- request: int32 [4, 15], replicated, may hold values from 0 to 15, as said below
- frame_pick: int32 [4, 15], replicated, may hold values from 0 to 7
- shift_rows: int32 [4, 15], replicated, may hold values from -1 to 1
- shift_cols: int32 [4, 15], replicated, may hold values from -1 to 1
- hist_count: int32 [4], replicated, may hold values from 1 to 15
- join_weight: bfloat16 [4096, 256], replicated, may hold values from -0.09375 to 0.09375
- conv_one: bfloat16 [2304, 256], replicated, may hold values from -0.125 to 0.125
- conv_two: bfloat16 [2304, 256], replicated, may hold values from -0.125 to 0.125
- grad_out: bfloat16 [4, 64, 32, 256], P('clip', 'row', 'col'), may hold values from -6 to 6
Outputs:
- encoded: bfloat16 [4, 64, 32, 256], P('clip', 'row', 'col')
- weight_grads: float32 [8704, 256], P(('clip', 'row'), 'col')
The draws below stay inside these ranges and needn't reach their ends.
Inputs may be any that keep to these rules, and one draw needn't show every extreme that they name: `request`: each row holds 15 different values; value v names source clip v // 4, so at most 4 slots of one clip come from one source clip.
All inputs are finite; a program needn't handle non-finite values.
Results may differ from the reference program's by a relative error of at most 0.012.
The reference program's roundings to bfloat16 on the way (of `warped`, `joined`, `act`, `hidden`, `d_conv1` and `d_joined`) count: a program that leaves them out, or rounds other values in their place, can miss the bound.
Values may be sent and summed in bfloat16 or wider, within the bound.
A program may use at most 128 MiB of HBM per device.

```python
import jax
import jax.numpy as jnp
from jax import lax

C = 256
HIST = 15
FRAMES = 8
TS = 8
CLIPS = 4
CAP = 4
NR = 64
NC = 32


def pick_two(key):
    first = jax.random.randint(jax.random.fold_in(key, 7), (), 0, CLIPS)
    second = (first + 1 + jax.random.randint(jax.random.fold_in(key, 8), (), 0, CLIPS - 1)) % CLIPS
    return (first, second)


def draw_request(key, part):
    total = CLIPS * CAP
    keys = jax.random.split(jax.random.fold_in(key, 3), CLIPS)
    perms = jax.vmap(lambda sub: jax.random.permutation(sub, total))(keys)[:, :HIST].astype(jnp.int32)
    first, second = pick_two(jax.random.fold_in(key, 11))
    clips = jnp.arange(CLIPS)
    offset = jnp.where(clips == first, total - 1 - perms[:, 0], jnp.where(clips == second, total - perms[:, 0], 0))
    return ((perms + offset[:, None]) % total).astype(jnp.int32)


def draw_hist_count(key, part):
    upper = jax.random.randint(jax.random.fold_in(key, 1), (CLIPS,), 1, HIST + 1)
    lower = jax.random.randint(jax.random.fold_in(key, 2), (CLIPS,), 1, HIST + 1)
    counts = jnp.minimum(upper, lower)
    first, second = pick_two(jax.random.fold_in(key, 13))
    clips = jnp.arange(CLIPS)
    counts = jnp.where(clips == first, HIST, jnp.where(clips == second, 1, counts))
    return counts.astype(jnp.int32)


def plant(entries, own_key, smallest, high):
    longest = entries.shape.index(max(entries.shape))
    spots = []
    for shift in (0, 1):
        where = [jax.random.randint(jax.random.fold_in(own_key, axis), (), 0, length) for axis, length in enumerate(entries.shape)]
        where[longest] = (where[longest] + shift) % entries.shape[longest]
        spots.append(tuple(where))
    return entries.at[spots[0]].set(smallest).at[spots[1]].set(high)


def block_levels(stream_key, extent, pieces, smallest, largest):
    loudness = 1.0
    for axis_at, parts in pieces:
        heights = jax.random.uniform(jax.random.fold_in(jax.random.fold_in(stream_key, 6), axis_at), (parts,), jnp.float32, smallest / len(pieces), largest / len(pieces))
        loudness = loudness * jnp.repeat(jnp.exp(heights), extent[axis_at] // parts).reshape((-1,) + (1,) * (len(extent) - 1 - axis_at))
    return loudness


def noise(rng, dims, scale, reach, pieces=(), kind=jnp.bfloat16):
    entries = jax.random.normal(rng, dims, jnp.float32) * scale
    if len(pieces) > 0:
        entries = block_levels(rng, dims, pieces, -0.22, 0.18) * entries
    return jnp.clip(entries, min=-reach, max=reach).astype(kind)


def setup_inputs(seed: int = 0) -> dict:
    streams_of = jax.random.split(jax.random.key(seed), 12)
    current = noise(streams_of[0], (CLIPS, NR, NC, C), 1.0, 6.0, ((0, 4), (1, 4), (2, 2)))
    bank = noise(streams_of[1], (CLIPS, FRAMES, NR, NC, C), 1.0, 6.0, ((0, 4), (2, 4), (3, 2)))
    request = draw_request(jax.random.fold_in(streams_of[11], 71), 0)
    frame_pick = plant(jax.random.randint(streams_of[3], (CLIPS, HIST), 0, FRAMES), jax.random.fold_in(streams_of[3], 1), 0, FRAMES - 1).astype(jnp.int32)
    shift_rows = plant(jax.random.randint(streams_of[4], (CLIPS, HIST), -1, 2), jax.random.fold_in(streams_of[4], 1), -1, 1).astype(jnp.int32)
    shift_cols = plant(jax.random.randint(streams_of[5], (CLIPS, HIST), -1, 2), jax.random.fold_in(streams_of[5], 1), -1, 1).astype(jnp.int32)
    hist_count = draw_hist_count(jax.random.fold_in(streams_of[11], 71), 0)
    join_weight = noise(streams_of[7], ((HIST + 1) * C, C), ((HIST + 1) * C) ** -0.5, 0.09375)
    conv_one = noise(streams_of[8], (9 * C, C), (9 * C) ** -0.5, 0.125)
    conv_two = noise(streams_of[9], (9 * C, C), (9 * C) ** -0.5, 0.125)
    grad_out = noise(streams_of[10], (CLIPS, NR, NC, C), 1.0, 6.0, ((0, 4), (1, 4), (2, 2)))
    return dict(current=current, bank=bank, request=request, frame_pick=frame_pick, shift_rows=shift_rows, shift_cols=shift_cols, hist_count=hist_count, join_weight=join_weight, conv_one=conv_one, conv_two=conv_two, grad_out=grad_out)


def shift_tile(tile, step_rows, step_cols):
    padded = jnp.pad(tile, ((TS, TS), (TS, TS), (0, 0)))
    start_row = ((1 - step_rows) * TS).astype(jnp.int32)
    start_col = ((1 - step_cols) * TS).astype(jnp.int32)
    return lax.dynamic_slice(padded, (start_row, start_col, jnp.int32(0)), (NR, NC, C))


def neighbourhood(field, mirror):
    padded = jnp.pad(field, ((1, 1), (1, 1), (0, 0)))
    views = []
    for row_tap in range(3):
        for col_tap in range(3):
            top = 2 - row_tap if mirror else row_tap
            left = 2 - col_tap if mirror else col_tap
            views.append(padded[top:top + NR, left:left + NC])
    return jnp.concatenate(views, axis=-1).reshape(NR * NC, 9 * C)


def flipped(weight):
    return weight.reshape(9, C, C).transpose(0, 2, 1).reshape(9 * C, C)


def reference(current, bank, request, frame_pick, shift_rows, shift_cols, hist_count, join_weight, conv_one, conv_two, grad_out):
    one_back = flipped(conv_one)
    two_back = flipped(conv_two)
    join_blocks = join_weight.reshape(HIST + 1, C, C).astype(jnp.float32)

    def per_clip(total, clip):
        source = request[clip] // CAP
        tiles = bank[source, frame_pick[clip]]
        warped = jax.vmap(shift_tile)(tiles, shift_rows[clip], shift_cols[clip])
        valid = (jnp.arange(HIST) < hist_count[clip]).astype(jnp.bfloat16)
        warped = warped * valid[:, None, None, None]
        stacked = jnp.concatenate([current[clip][None], warped], axis=0).reshape(HIST + 1, NR * NC, C)
        joined = jnp.einsum("kpc,kcd->pd", stacked.astype(jnp.float32), join_blocks).astype(jnp.bfloat16)
        act = jnp.maximum(joined, 0)
        act_patch = neighbourhood(act.reshape(NR, NC, C), False)
        conv1 = jnp.dot(act_patch, conv_one, preferred_element_type=jnp.float32)
        hidden = jnp.maximum(conv1, 0.0).astype(jnp.bfloat16)
        hidden_patch = neighbourhood(hidden.reshape(NR, NC, C), False)
        conv2 = jnp.dot(hidden_patch, conv_two, preferred_element_type=jnp.float32)
        encoded = (joined.astype(jnp.float32) + conv2).astype(jnp.bfloat16)
        upstream = grad_out[clip]
        flat_up = upstream.reshape(NR * NC, C)
        grad_two = jnp.dot(hidden_patch.T, flat_up, preferred_element_type=jnp.float32)
        d_hidden = jnp.dot(neighbourhood(upstream, True), two_back, preferred_element_type=jnp.float32)
        d_conv1 = jnp.where(conv1 > 0, d_hidden, 0.0).astype(jnp.bfloat16)
        grad_one = jnp.dot(act_patch.T, d_conv1, preferred_element_type=jnp.float32)
        d_act = jnp.dot(neighbourhood(d_conv1.reshape(NR, NC, C), True), one_back, preferred_element_type=jnp.float32)
        d_joined = (flat_up.astype(jnp.float32) + jnp.where(joined > 0, d_act, 0.0)).astype(jnp.bfloat16)
        grad_join = jnp.einsum("kpc,pd->kcd", stacked.astype(jnp.float32), d_joined.astype(jnp.float32)).reshape((HIST + 1) * C, C)
        term = jnp.concatenate([grad_join, grad_one, grad_two], axis=0)
        return total + term, encoded.reshape(NR, NC, C)

    start = jnp.zeros(((HIST + 19) * C, C), jnp.float32)
    weight_grads, encoded = lax.scan(per_clip, start, jnp.arange(CLIPS))
    return encoded, weight_grads
```

```python
import jax
import jax.numpy as jnp
from jax import lax
from jax.sharding import PartitionSpec as P

HIST = 15
TS = 8


def extended(block, sides, width):
    for axis, dim in sides:
        count = lax.axis_size(axis)
        forward = [(i, i + 1) for i in range(count - 1)]
        backward = [(target, source) for source, target in forward]
        low = lax.ppermute(
            lax.slice_in_dim(block, block.shape[dim] - width, None, axis=dim), axis, forward
        )
        high = lax.ppermute(lax.slice_in_dim(block, 0, width, axis=dim), axis, backward)
        block = jnp.concatenate([low, block, high], axis=dim)
    return block


def tap_views(padded, height, width, mirror):
    views = []
    for row_tap in range(3):
        for col_tap in range(3):
            top = 2 - row_tap if mirror else row_tap
            left = 2 - col_tap if mirror else col_tap
            views.append(padded[top : top + height, left : left + width])
    return jnp.concatenate(views, axis=-1).reshape(height * width, -1)


def forward_patch(field):
    padded = extended(field, (("row", 0), ("col", 1)), 1)
    return tap_views(padded, field.shape[0], field.shape[1], False)


def backward_patch(field):
    padded = extended(field, (("row", 0), ("col", 1)), 1)
    return tap_views(padded, field.shape[0], field.shape[1], True)


def flipped(weight):
    channels = weight.shape[1]
    return weight.reshape(9, channels, channels).transpose(0, 2, 1).reshape(9 * channels, channels)


def window_cut(padded, step_rows, step_cols, height, width, tile):
    start_row = (1 - step_rows) * tile
    start_col = (1 - step_cols) * tile
    zero = jnp.int32(0)
    return lax.dynamic_slice(padded, (start_row, start_col, zero), (height, width, padded.shape[2]))


def local(
    current,
    bank,
    request,
    frame_pick,
    shift_rows,
    shift_cols,
    hist_count,
    join_weight,
    conv_one,
    conv_two,
    grad_out,
):
    height, width, channels = (current.shape[1], current.shape[2], current.shape[3])
    clip_count = lax.axis_size("clip")
    capacity = (HIST + clip_count - 1) // clip_count
    own_clip = lax.axis_index("clip")
    slot_ids = own_clip * capacity + jnp.arange(capacity, dtype=jnp.int32)
    matches = (request[:, None, :] == slot_ids[None, :, None]).astype(jnp.int32)
    chosen = jnp.sum(matches * frame_pick[:, None, :], axis=-1).reshape(-1)
    served = jnp.sum(matches, axis=-1).reshape(-1).astype(jnp.bfloat16)
    own_request = lax.dynamic_index_in_dim(request, own_clip, 0, False)
    own_rows = lax.dynamic_index_in_dim(shift_rows, own_clip, 0, False)
    own_cols = lax.dynamic_index_in_dim(shift_cols, own_clip, 0, False)
    own_count = lax.dynamic_index_in_dim(hist_count, own_clip, 0, False)
    frames = bank[0]
    outgoing = jnp.take(frames, chosen, axis=0) * served[:, None, None, None]
    outgoing = outgoing.reshape(clip_count, capacity, height, width, channels)
    received = lax.all_to_all(outgoing, "clip", split_axis=0, concat_axis=0, tiled=True)
    fetched = jnp.take(
        received.reshape(clip_count * capacity, height, width, channels), own_request, axis=0
    )
    padded_slots = extended(fetched, (("row", 1), ("col", 2)), TS)
    warped = jax.vmap(
        lambda slot, step_rows, step_cols: window_cut(slot, step_rows, step_cols, height, width, TS)
    )(padded_slots, own_rows, own_cols)
    valid = (jnp.arange(HIST) < own_count).astype(jnp.bfloat16)
    warped = warped * valid[:, None, None, None]
    cells = height * width
    stacked = jnp.concatenate([current[0][None], warped], axis=0).reshape(HIST + 1, cells, channels)
    join_blocks = join_weight.reshape(HIST + 1, channels, channels)
    joined = jnp.einsum(
        "kpc,kcd->pd", stacked, join_blocks, preferred_element_type=jnp.float32
    ).astype(jnp.bfloat16)
    act = jnp.maximum(joined, 0)
    act_patch = forward_patch(act.reshape(height, width, channels))
    conv1 = jnp.dot(act_patch, conv_one, preferred_element_type=jnp.float32)
    hidden = jnp.maximum(conv1, 0.0).astype(jnp.bfloat16)
    hidden_patch = forward_patch(hidden.reshape(height, width, channels))
    conv2 = jnp.dot(hidden_patch, conv_two, preferred_element_type=jnp.float32)
    encoded = (
        (joined.astype(jnp.float32) + conv2)
        .astype(jnp.bfloat16)
        .reshape(1, height, width, channels)
    )
    upstream = grad_out[0]
    flat_up = upstream.reshape(cells, channels)
    grad_two = jnp.dot(hidden_patch.T, flat_up, preferred_element_type=jnp.float32)
    d_hidden = jnp.dot(
        backward_patch(upstream), flipped(conv_two), preferred_element_type=jnp.float32
    )
    d_conv1 = jnp.where(conv1 > 0, d_hidden, 0.0).astype(jnp.bfloat16)
    grad_one = jnp.dot(act_patch.T, d_conv1, preferred_element_type=jnp.float32)
    d_act = jnp.dot(
        backward_patch(d_conv1.reshape(height, width, channels)),
        flipped(conv_one),
        preferred_element_type=jnp.float32,
    )
    d_joined = (flat_up.astype(jnp.float32) + jnp.where(joined > 0, d_act, 0.0)).astype(
        jnp.bfloat16
    )
    grad_join = jnp.einsum(
        "kpc,pd->kcd", stacked, d_joined, preferred_element_type=jnp.float32
    ).reshape((HIST + 1) * channels, channels)
    term = jnp.concatenate([grad_join, grad_one, grad_two], axis=0)
    shared = lax.psum_scatter(
        term.astype(jnp.bfloat16), "col", scatter_dimension=1, tiled=True
    )
    weight_grads = lax.psum_scatter(
        shared, ("clip", "row"), scatter_dimension=0, tiled=True
    ).astype(jnp.float32)
    return (encoded, weight_grads)


def solution(mesh):
    placed = (
        P("clip", "row", "col", None),
        P("clip", None, "row", "col", None),
        P(),
        P(),
        P(),
        P(),
        P(),
        P(),
        P(),
        P(),
        P("clip", "row", "col", None),
    )
    return jax.shard_map(
        local,
        mesh=mesh,
        in_specs=placed,
        out_specs=(P("clip", "row", "col", None), P(("clip", "row"), "col")),
        check_vma=False,
    )
```

```python
import jax
import jax.numpy as jnp
from jax import lax
from jax.experimental import pallas as pl
from jax.experimental.pallas import tpu as pltpu
from jax.sharding import PartitionSpec as P

HIST = 15


def extended(block, sides, width):
    for axis, dim in sides:
        count = lax.axis_size(axis)
        forward = [(i, i + 1) for i in range(count - 1)]
        backward = [(target, source) for source, target in forward]
        low = lax.ppermute(
            lax.slice_in_dim(block, block.shape[dim] - width, None, axis=dim), axis, forward
        )
        high = lax.ppermute(lax.slice_in_dim(block, 0, width, axis=dim), axis, backward)
        block = jnp.concatenate([low, block, high], axis=dim)
    return block


def fetch_kernel(
    served, wanted, bank, out, own, rim, chosen, got, near_sem, row_sem, col_sem, clip_sem, local_sem
):
    frames = bank.shape[0]
    clips = lax.axis_size("clip")
    rows = lax.axis_size("row")
    cols = lax.axis_size("col")
    capacity = got.shape[1] // clips
    clip = lax.axis_index("clip")
    row = lax.axis_index("row")
    col = lax.axis_index("col")
    up, down, left, right = row > 0, row < rows - 1, col > 0, col < cols - 1

    def signal(**where):
        pl.semaphore_signal(
            pltpu.get_barrier_semaphore(), inc=1, device_id=where, device_id_type=pl.DeviceIdType.MESH
        )

    def remote(source, target, sems, where):
        return pltpu.make_async_remote_copy(
            src_ref=source,
            dst_ref=target,
            send_sem=sems.at[0],
            recv_sem=sems.at[1],
            device_id=where,
            device_id_type=pl.DeviceIdType.MESH,
        )

    centre = pltpu.make_async_copy(bank, own.at[0:frames, :, :, 1:3], local_sem)
    centre.start()
    partners = [lax.rem(clip + step, clips) for step in range(1, clips)]
    for partner in partners:
        signal(clip=partner)
    for there, axis, index in (
        (up, "row", row - 1),
        (down, "row", row + 1),
        (left, "col", col - 1),
        (right, "col", col + 1),
    ):
        pl.when(there)(lambda axis=axis, index=index: signal(**{axis: index}))
    peers = clips - 1
    for there in (up, down, left, right):
        peers = peers + there.astype(jnp.int32)
    pl.semaphore_wait(pltpu.get_barrier_semaphore(), peers)

    to_right = remote(bank.at[:, :, :, 1], own.at[0:frames, :, :, 0], near_sem.at[0], {"col": col + 1})
    to_left = remote(bank.at[:, :, :, 0], own.at[0:frames, :, :, 3], near_sem.at[1], {"col": col - 1})
    to_down = remote(bank.at[:, 1], rim.at[0:frames, 0, :, 1:3], row_sem.at[0], {"row": row + 1})
    to_up = remote(bank.at[:, 0], rim.at[0:frames, 2, :, 1:3], row_sem.at[1], {"row": row - 1})
    pl.when(right)(to_right.start)
    pl.when(left)(to_left.start)
    pl.when(down)(to_down.start)
    pl.when(up)(to_up.start)

    own[frames] = jnp.zeros_like(own[frames])
    rim[frames] = jnp.zeros_like(rim[frames])

    def clear(view, place):
        for frame in range(frames):
            view[(frame,) + place] = jnp.zeros_like(view[(frame,) + place])

    every = slice(None)
    pl.when(jnp.logical_not(up))(lambda: clear(rim, (0,)))
    pl.when(jnp.logical_not(down))(lambda: clear(rim, (2,)))

    @pl.when(jnp.logical_not(left))
    def _():
        clear(own, (every, every, 0))
        clear(rim, (0, every, 0))
        clear(rim, (2, every, 0))

    @pl.when(jnp.logical_not(right))
    def _():
        clear(own, (every, every, 3))
        clear(rim, (0, every, 3))
        clear(rim, (2, every, 3))

    centre.wait()
    pl.when(left)(to_right.wait_recv)
    pl.when(right)(to_left.wait_recv)

    def decode(slot):
        packed = served[slot]
        shift_col = lax.rem(packed, 3) - 1
        rest = lax.div(packed, 3)
        return lax.div(rest, 3), lax.rem(rest, 3) - 1, shift_col

    def pick(part, target, partner):
        for spot in range(capacity):
            slot = partner * capacity + spot
            frame, shift_row, shift_col = decode(slot)
            if part == 0:
                line = jnp.where(shift_row < 0, 1, 0)
                target[0, slot] = own[frame, line, :, pl.ds(1 - shift_col, 2)]
            else:
                target[1, slot] = rim[frame, 1 - shift_row, :, pl.ds(1 - shift_col, 2)]

    sends = []

    def send(part, step):
        copy = remote(
            chosen.at[part, pl.ds(partners[step - 1] * capacity, capacity)],
            got.at[part, pl.ds(clip * capacity, capacity)],
            clip_sem.at[part, step - 1],
            {"clip": partners[step - 1]},
        )
        copy.start()
        sends.append(copy)

    for part in range(2):
        if part == 1:
            def keep(frame, carry):
                rim[frame, 1] = own[frame, 1]
                return carry

            lax.fori_loop(0, frames, keep, 0)
            pl.when(up)(to_down.wait_recv)
            pl.when(down)(to_up.wait_recv)
            corners = [
                (up, right, remote(rim.at[0:frames, 0, :, 2], rim.at[0:frames, 0, :, 0], col_sem.at[0], {"col": col + 1})),
                (down, right, remote(rim.at[0:frames, 2, :, 2], rim.at[0:frames, 2, :, 0], col_sem.at[1], {"col": col + 1})),
                (up, left, remote(rim.at[0:frames, 0, :, 1], rim.at[0:frames, 0, :, 3], col_sem.at[2], {"col": col - 1})),
                (down, left, remote(rim.at[0:frames, 2, :, 1], rim.at[0:frames, 2, :, 3], col_sem.at[3], {"col": col - 1})),
            ]
            for vertical, side, copy in corners:
                pl.when(jnp.logical_and(vertical, side))(copy.start)
            for (vertical, _, copy), other in zip(corners, (left, left, right, right)):
                pl.when(jnp.logical_and(vertical, other))(copy.wait_recv)
        for step in range(1, clips):
            pick(part, chosen, partners[step - 1])
            if step > 1:
                send(part, step - 1)
        pick(part, got, clip)
        send(part, clips - 1)
    for copy in sends:
        copy.wait_recv()
    slots = out.shape[0]
    for slot in range(slots):
        packed = wanted[slot]
        place = lax.div(packed, 2)
        flag = lax.rem(packed, 2)
        out[slot, 0] = got[flag, place]
        out[slot, 1] = got[1 - flag, place]
    for copy in sends:
        copy.wait_send()
    pl.when(right)(to_right.wait_send)
    pl.when(left)(to_left.wait_send)
    pl.when(down)(to_down.wait_send)
    pl.when(up)(to_up.wait_send)
    for vertical, side, copy in corners:
        pl.when(jnp.logical_and(vertical, side))(copy.wait_send)


def fetch(bank, request, frame_pick, shift_rows, shift_cols, hist_count):
    frames, height, width, channels = bank.shape
    clips = lax.axis_size("clip")
    capacity = (HIST + clips - 1) // clips
    own_clip = lax.axis_index("clip")
    slot_ids = own_clip * capacity + jnp.arange(capacity, dtype=jnp.int32)
    matches = (request[:, None, :] == slot_ids[None, :, None]).astype(jnp.int32)
    valid = jnp.arange(HIST)[None, :] < hist_count[:, None]
    frame = jnp.where(valid, frame_pick, frames)
    packed = (frame * 3 + shift_rows + 1) * 3 + shift_cols + 1
    served = jnp.sum(matches * packed[:, None, :], axis=-1).reshape(-1)
    pair = request * 2 + (shift_rows == 1).astype(jnp.int32)
    wanted = lax.dynamic_index_in_dim(pair, own_clip, 0, False)
    half = (height // 2, 2, width // 2, channels)
    blocks = bank.reshape((frames, 2) + half)
    wide = (height // 2, 4, width // 2, channels)
    smem = pl.BlockSpec(memory_space=pltpu.SMEM)
    dma = pltpu.SemaphoreType.DMA
    out = pl.pallas_call(
        fetch_kernel,
        out_shape=jax.ShapeDtypeStruct((HIST, 2) + half, bank.dtype),
        in_specs=[smem, smem, pl.BlockSpec(memory_space=pl.ANY)],
        out_specs=pl.BlockSpec(memory_space=pltpu.VMEM),
        scratch_shapes=[
            pltpu.VMEM((frames + 1, 2) + wide, bank.dtype),
            pltpu.VMEM((frames + 1, 3) + wide, bank.dtype),
            pltpu.VMEM((2, clips * capacity) + half, bank.dtype),
            pltpu.VMEM((2, clips * capacity) + half, bank.dtype),
            dma((2, 2)),
            dma((2, 2)),
            dma((4, 2)),
            dma((2, clips - 1, 2)),
            dma,
        ],
        compiler_params=pltpu.CompilerParams(
            collective_id=0, has_side_effects=True, vmem_limit_bytes=40 * 1024 * 1024
        ),
        name="fetch",
    )(served, wanted, blocks)
    return out.reshape(HIST, height * width, channels)


def tap_views(padded, height, width, mirror):
    views = []
    for row_tap in range(3):
        for col_tap in range(3):
            top = 2 - row_tap if mirror else row_tap
            left = 2 - col_tap if mirror else col_tap
            views.append(padded[top : top + height, left : left + width])
    return jnp.concatenate(views, axis=-1).reshape(height * width, -1)


def forward_patch(field):
    padded = extended(field, (("row", 0), ("col", 1)), 1)
    return tap_views(padded, field.shape[0], field.shape[1], False)


def backward_patch(field):
    padded = extended(field, (("row", 0), ("col", 1)), 1)
    return tap_views(padded, field.shape[0], field.shape[1], True)


def flipped(weight):
    channels = weight.shape[1]
    return weight.reshape(9, channels, channels).transpose(0, 2, 1).reshape(9 * channels, channels)


def local(
    current,
    bank,
    request,
    frame_pick,
    shift_rows,
    shift_cols,
    hist_count,
    join_weight,
    conv_one,
    conv_two,
    grad_out,
):
    height, width, channels = (current.shape[1], current.shape[2], current.shape[3])
    warped = fetch(bank[0], request, frame_pick, shift_rows, shift_cols, hist_count)
    cells = height * width
    stacked = jnp.concatenate([current.reshape(1, cells, channels), warped], axis=0)
    join_blocks = join_weight.reshape(HIST + 1, channels, channels)
    joined = jnp.einsum(
        "kpc,kcd->pd", stacked, join_blocks, preferred_element_type=jnp.float32
    ).astype(jnp.bfloat16)
    act = jnp.maximum(joined, 0)
    act_patch = forward_patch(act.reshape(height, width, channels))
    conv1 = jnp.dot(act_patch, conv_one, preferred_element_type=jnp.float32)
    hidden = jnp.maximum(conv1, 0.0).astype(jnp.bfloat16)
    hidden_patch = forward_patch(hidden.reshape(height, width, channels))
    conv2 = jnp.dot(hidden_patch, conv_two, preferred_element_type=jnp.float32)
    encoded = (
        (joined.astype(jnp.float32) + conv2)
        .astype(jnp.bfloat16)
        .reshape(1, height, width, channels)
    )
    upstream = grad_out[0]
    flat_up = upstream.reshape(cells, channels)
    grad_two = jnp.dot(hidden_patch.T, flat_up, preferred_element_type=jnp.float32)
    d_hidden = jnp.dot(
        backward_patch(upstream), flipped(conv_two), preferred_element_type=jnp.float32
    )
    d_conv1 = jnp.where(conv1 > 0, d_hidden, 0.0).astype(jnp.bfloat16)
    grad_one = jnp.dot(act_patch.T, d_conv1, preferred_element_type=jnp.float32)
    d_act = jnp.dot(
        backward_patch(d_conv1.reshape(height, width, channels)),
        flipped(conv_one),
        preferred_element_type=jnp.float32,
    )
    d_joined = (flat_up.astype(jnp.float32) + jnp.where(joined > 0, d_act, 0.0)).astype(
        jnp.bfloat16
    )
    grad_join = jnp.einsum(
        "kpc,pd->kcd", stacked, d_joined, preferred_element_type=jnp.float32
    ).reshape((HIST + 1) * channels, channels)
    term = jnp.concatenate([grad_join, grad_one, grad_two], axis=0)
    shared = lax.psum_scatter(
        term.astype(jnp.bfloat16), "col", scatter_dimension=1, tiled=True
    )
    weight_grads = lax.psum_scatter(
        shared, ("clip", "row"), scatter_dimension=0, tiled=True
    ).astype(jnp.float32)
    return (encoded, weight_grads)


def solution(mesh):
    placed = (
        P("clip", "row", "col", None),
        P("clip", None, "row", "col", None),
        P(),
        P(),
        P(),
        P(),
        P(),
        P(),
        P(),
        P(),
        P("clip", "row", "col", None),
    )
    return jax.shard_map(
        local,
        mesh=mesh,
        in_specs=placed,
        out_specs=(P("clip", "row", "col", None), P(("clip", "row"), "col")),
        check_vma=False,
    )
```

```python
import jax
import jax.numpy as jnp
from jax import lax
from jax.experimental import pallas as pl
from jax.experimental.pallas import tpu as pltpu
from jax.sharding import PartitionSpec as P

HIST = 15


def extended(block, sides, width):
    for axis, dim in sides:
        count = lax.axis_size(axis)
        forward = [(i, i + 1) for i in range(count - 1)]
        backward = [(target, source) for source, target in forward]
        low = lax.ppermute(
            lax.slice_in_dim(block, block.shape[dim] - width, None, axis=dim), axis, forward
        )
        high = lax.ppermute(lax.slice_in_dim(block, 0, width, axis=dim), axis, backward)
        block = jnp.concatenate([low, block, high], axis=dim)
    return block


def fetch_kernel(
    served, wanted, bank, out, own, rim, chosen, got, near_sem, row_sem, col_sem, clip_sem, local_sem
):
    frames = bank.shape[0]
    clips = lax.axis_size("clip")
    rows = lax.axis_size("row")
    cols = lax.axis_size("col")
    capacity = got.shape[1] // clips
    clip = lax.axis_index("clip")
    row = lax.axis_index("row")
    col = lax.axis_index("col")
    up, down, left, right = row > 0, row < rows - 1, col > 0, col < cols - 1

    def signal(**where):
        pl.semaphore_signal(
            pltpu.get_barrier_semaphore(), inc=1, device_id=where, device_id_type=pl.DeviceIdType.MESH
        )

    def remote(source, target, sems, where):
        return pltpu.make_async_remote_copy(
            src_ref=source,
            dst_ref=target,
            send_sem=sems.at[0],
            recv_sem=sems.at[1],
            device_id=where,
            device_id_type=pl.DeviceIdType.MESH,
        )

    centre = pltpu.make_async_copy(bank, own.at[0:frames, :, :, 1:3], local_sem)
    centre.start()
    partners = [lax.rem(clip + step, clips) for step in range(1, clips)]
    for partner in partners:
        signal(clip=partner)
    for there, axis, index in (
        (up, "row", row - 1),
        (down, "row", row + 1),
        (left, "col", col - 1),
        (right, "col", col + 1),
    ):
        pl.when(there)(lambda axis=axis, index=index: signal(**{axis: index}))
    peers = clips - 1
    for there in (up, down, left, right):
        peers = peers + there.astype(jnp.int32)
    pl.semaphore_wait(pltpu.get_barrier_semaphore(), peers)

    to_right = remote(bank.at[:, :, :, 1], own.at[0:frames, :, :, 0], near_sem.at[0], {"col": col + 1})
    to_left = remote(bank.at[:, :, :, 0], own.at[0:frames, :, :, 3], near_sem.at[1], {"col": col - 1})
    to_down = remote(bank.at[:, 1], rim.at[0:frames, 0, :, 1:3], row_sem.at[0], {"row": row + 1})
    to_up = remote(bank.at[:, 0], rim.at[0:frames, 2, :, 1:3], row_sem.at[1], {"row": row - 1})
    pl.when(right)(to_right.start)
    pl.when(left)(to_left.start)
    pl.when(down)(to_down.start)
    pl.when(up)(to_up.start)

    own[frames] = jnp.zeros_like(own[frames])
    rim[frames] = jnp.zeros_like(rim[frames])

    def clear(view, place):
        for frame in range(frames):
            view[(frame,) + place] = jnp.zeros_like(view[(frame,) + place])

    every = slice(None)
    pl.when(jnp.logical_not(up))(lambda: clear(rim, (0,)))
    pl.when(jnp.logical_not(down))(lambda: clear(rim, (2,)))

    @pl.when(jnp.logical_not(left))
    def _():
        clear(own, (every, every, 0))
        clear(rim, (0, every, 0))
        clear(rim, (2, every, 0))

    @pl.when(jnp.logical_not(right))
    def _():
        clear(own, (every, every, 3))
        clear(rim, (0, every, 3))
        clear(rim, (2, every, 3))

    centre.wait()
    pl.when(left)(to_right.wait_recv)
    pl.when(right)(to_left.wait_recv)

    def decode(slot):
        packed = served[slot]
        shift_col = lax.rem(packed, 3) - 1
        rest = lax.div(packed, 3)
        return lax.div(rest, 3), lax.rem(rest, 3) - 1, shift_col

    def pick(part, target, partner):
        for spot in range(capacity):
            slot = partner * capacity + spot
            frame, shift_row, shift_col = decode(slot)
            if part == 0:
                line = jnp.where(shift_row < 0, 1, 0)
                target[0, slot] = own[frame, line, :, pl.ds(1 - shift_col, 2)]
            else:
                target[1, slot] = rim[frame, 1 - shift_row, :, pl.ds(1 - shift_col, 2)]

    sends = []

    def send(part, step):
        copy = remote(
            chosen.at[part, pl.ds(partners[step - 1] * capacity, capacity)],
            got.at[part, pl.ds(clip * capacity, capacity)],
            clip_sem.at[part, step - 1],
            {"clip": partners[step - 1]},
        )
        copy.start()
        sends.append(copy)

    for part in range(2):
        if part == 1:
            def keep(frame, carry):
                rim[frame, 1] = own[frame, 1]
                return carry

            lax.fori_loop(0, frames, keep, 0)
            pl.when(up)(to_down.wait_recv)
            pl.when(down)(to_up.wait_recv)
            corners = [
                (up, right, remote(rim.at[0:frames, 0, :, 2], rim.at[0:frames, 0, :, 0], col_sem.at[0], {"col": col + 1})),
                (down, right, remote(rim.at[0:frames, 2, :, 2], rim.at[0:frames, 2, :, 0], col_sem.at[1], {"col": col + 1})),
                (up, left, remote(rim.at[0:frames, 0, :, 1], rim.at[0:frames, 0, :, 3], col_sem.at[2], {"col": col - 1})),
                (down, left, remote(rim.at[0:frames, 2, :, 1], rim.at[0:frames, 2, :, 3], col_sem.at[3], {"col": col - 1})),
            ]
            for vertical, side, copy in corners:
                pl.when(jnp.logical_and(vertical, side))(copy.start)
            for (vertical, _, copy), other in zip(corners, (left, left, right, right)):
                pl.when(jnp.logical_and(vertical, other))(copy.wait_recv)
        for step in range(1, clips):
            pick(part, chosen, partners[step - 1])
            if step > 1:
                send(part, step - 1)
        pick(part, got, clip)
        send(part, clips - 1)
    for copy in sends:
        copy.wait_recv()
    slots = out.shape[0]
    for slot in range(slots):
        packed = wanted[slot]
        place = lax.div(packed, 2)
        flag = lax.rem(packed, 2)
        out[slot, 0] = got[flag, place]
        out[slot, 1] = got[1 - flag, place]
    for copy in sends:
        copy.wait_send()
    pl.when(right)(to_right.wait_send)
    pl.when(left)(to_left.wait_send)
    pl.when(down)(to_down.wait_send)
    pl.when(up)(to_up.wait_send)
    for vertical, side, copy in corners:
        pl.when(jnp.logical_and(vertical, side))(copy.wait_send)


def fetch(bank, request, frame_pick, shift_rows, shift_cols, hist_count):
    frames, height, width, channels = bank.shape
    clips = lax.axis_size("clip")
    capacity = (HIST + clips - 1) // clips
    own_clip = lax.axis_index("clip")
    slot_ids = own_clip * capacity + jnp.arange(capacity, dtype=jnp.int32)
    matches = (request[:, None, :] == slot_ids[None, :, None]).astype(jnp.int32)
    valid = jnp.arange(HIST)[None, :] < hist_count[:, None]
    frame = jnp.where(valid, frame_pick, frames)
    packed = (frame * 3 + shift_rows + 1) * 3 + shift_cols + 1
    served = jnp.sum(matches * packed[:, None, :], axis=-1).reshape(-1)
    pair = request * 2 + (shift_rows == 1).astype(jnp.int32)
    wanted = lax.dynamic_index_in_dim(pair, own_clip, 0, False)
    half = (height // 2, 2, width // 2, channels)
    blocks = bank.reshape((frames, 2) + half)
    wide = (height // 2, 4, width // 2, channels)
    smem = pl.BlockSpec(memory_space=pltpu.SMEM)
    dma = pltpu.SemaphoreType.DMA
    out = pl.pallas_call(
        fetch_kernel,
        out_shape=jax.ShapeDtypeStruct((HIST, 2) + half, bank.dtype),
        in_specs=[smem, smem, pl.BlockSpec(memory_space=pl.ANY)],
        out_specs=pl.BlockSpec(memory_space=pltpu.VMEM),
        scratch_shapes=[
            pltpu.VMEM((frames + 1, 2) + wide, bank.dtype),
            pltpu.VMEM((frames + 1, 3) + wide, bank.dtype),
            pltpu.VMEM((2, clips * capacity) + half, bank.dtype),
            pltpu.VMEM((2, clips * capacity) + half, bank.dtype),
            dma((2, 2)),
            dma((2, 2)),
            dma((4, 2)),
            dma((2, clips - 1, 2)),
            dma,
        ],
        compiler_params=pltpu.CompilerParams(
            collective_id=0, has_side_effects=True, vmem_limit_bytes=40 * 1024 * 1024
        ),
        name="fetch",
    )(served, wanted, blocks)
    return out.reshape(HIST, height * width, channels)


def tap_views(padded, height, width, mirror):
    views = []
    for row_tap in range(3):
        for col_tap in range(3):
            top = 2 - row_tap if mirror else row_tap
            left = 2 - col_tap if mirror else col_tap
            views.append(padded[top : top + height, left : left + width])
    return jnp.stack(views).reshape(9, height * width, -1)


def forward_patch(field):
    padded = extended(field, (("row", 0), ("col", 1)), 1)
    return tap_views(padded, field.shape[0], field.shape[1], False)


def backward_patch(field):
    padded = extended(field, (("row", 0), ("col", 1)), 1)
    return tap_views(padded, field.shape[0], field.shape[1], True)


def flipped(weight):
    channels = weight.shape[1]
    return weight.reshape(9, channels, channels).transpose(0, 2, 1)


def flip(index, bit):
    return index + bit - 2 * bit * lax.rem(lax.div(index, bit), 2)


def gradient_kernel(
    counts, lhs, rhs, out, term, near_out, near_in, far_out, far_in, last_out, last_in, clip_out, clip_in,
    near_sem, far_sem, last_sem, clip_sem
):
    clips = lax.axis_size("clip")
    rows = lax.axis_size("row")
    clip = lax.axis_index("clip")
    row = lax.axis_index("row")
    col = lax.axis_index("col")
    bits = (1, 2)
    peers = [{"col": 1 - col}] + [{"row": flip(row, bit)} for bit in bits]
    peers += [{"clip": lax.rem(clip + step, clips)} for step in range(1, clips)]
    for where in peers:
        pl.semaphore_signal(
            pltpu.get_barrier_semaphore(), inc=1, device_id=where, device_id_type=pl.DeviceIdType.MESH
        )
    pl.semaphore_wait(pltpu.get_barrier_semaphore(), len(peers))

    def remote(source, target, sems, where):
        return pltpu.make_async_remote_copy(
            src_ref=source,
            dst_ref=target,
            send_sem=sems.at[0],
            recv_sem=sems.at[1],
            device_id=where,
            device_id_type=pl.DeviceIdType.MESH,
        )

    size = lhs.shape[2]
    lanes = term.shape[4]
    part_rows = term.shape[3]
    index = 0
    for group, count in enumerate(counts):
        for _ in range(count):
            product = lax.dot_general(
                lhs[index], rhs[group], (((0,), (0,)), ((), ())), preferred_element_type=jnp.float32
            )
            start = index * size
            done = 0
            while done < size:
                place = start + done
                piece = place // part_rows
                inside = place % part_rows
                length = min(size - done, part_rows - inside)
                for side in range(2):
                    term[side, piece // 2, piece % 2, inside : inside + length] = product[
                        done : done + length, side * lanes : (side + 1) * lanes
                    ]
                done += length
            index += 1

    order = [lax.rem(clip + step, clips) for step in range(1, clips)] + [clip]
    near = []
    for turn, target in enumerate(order):
        for spot in range(rows):
            block = target * rows + spot
            near_out[block] = term[1 - col, block].astype(near_out.dtype)
        near.append(
            remote(
                near_out.at[pl.ds(target * rows, rows)],
                near_in.at[pl.ds(target * rows, rows)],
                near_sem.at[turn],
                {"col": 1 - col},
            )
        )
        near[-1].start()

    def near_sum(turn, part, offset):
        spot = row
        for bit in bits:
            if offset & bit:
                spot = flip(spot, bit)
        block = order[turn] * rows + spot
        return term[col, block, part] + near_in[block, part].astype(jnp.float32)

    far, last, final = {}, {}, []

    def first(turn):
        near[turn].wait_recv()
        for part in range(2):
            one, two = bits if part == 0 else bits[::-1]
            for spot, offset in enumerate((one, one + two)):
                far_out[turn, part, spot] = near_sum(turn, part, offset).astype(far_out.dtype)
            far[turn, part] = remote(
                far_out.at[turn, part], far_in.at[turn, part], far_sem.at[turn, part], {"row": flip(row, one)}
            )
            far[turn, part].start()

    def second(turn):
        for part in range(2):
            one, two = bits if part == 0 else bits[::-1]
            far[turn, part].wait_recv()
            total = near_sum(turn, part, two) + far_in[turn, part, 1].astype(jnp.float32)
            last_out[turn, part] = total.astype(last_out.dtype)
            last[turn, part] = remote(
                last_out.at[turn, part], last_in.at[turn, part], last_sem.at[turn, part], {"row": flip(row, two)}
            )
            last[turn, part].start()

    def third(turn):
        for part in range(2):
            last[turn, part].wait_recv()
            total = near_sum(turn, part, 0) + far_in[turn, part, 0].astype(jnp.float32)
            total = total + last_in[turn, part].astype(jnp.float32)
            if turn < clips - 1:
                clip_out[turn, part] = total.astype(clip_out.dtype)
            else:
                out[part] = total
        if turn < clips - 1:
            copy = remote(clip_out.at[turn], clip_in.at[turn], clip_sem.at[turn], {"clip": order[turn]})
            copy.start()
            final.append(copy)

    for turn in range(clips + 2):
        if turn < clips:
            first(turn)
        if 0 <= turn - 1 < clips:
            second(turn - 1)
        if turn >= 2:
            third(turn - 2)
    for turn, copy in enumerate(final):
        copy.wait_recv()
        for part in range(2):
            out[part] += clip_in[turn, part].astype(jnp.float32)
    for copy in near + list(far.values()) + list(last.values()) + final:
        copy.wait_send()


def gradients(groups):
    lhs = jnp.concatenate([group[0] for group in groups], axis=0)
    rhs = jnp.stack([group[1] for group in groups])
    counts = tuple(group[0].shape[0] for group in groups)
    clips = lax.axis_size("clip")
    rows = lax.axis_size("row")
    total = lhs.shape[0] * lhs.shape[2]
    part_rows = total // (2 * clips * rows)
    lanes = rhs.shape[2] // lax.axis_size("col")
    piece = (part_rows, lanes)
    vmem = pl.BlockSpec(memory_space=pltpu.VMEM)
    dma = pltpu.SemaphoreType.DMA
    out = pl.pallas_call(
        lambda *refs: gradient_kernel(counts, *refs),
        out_shape=jax.ShapeDtypeStruct((2,) + piece, jnp.float32),
        in_specs=[vmem, vmem],
        out_specs=vmem,
        scratch_shapes=[
            pltpu.VMEM((2, clips * rows, 2) + piece, jnp.float32),
            pltpu.VMEM((clips * rows, 2) + piece, jnp.bfloat16),
            pltpu.VMEM((clips * rows, 2) + piece, jnp.bfloat16),
            pltpu.VMEM((clips, 2, rows // 2) + piece, jnp.bfloat16),
            pltpu.VMEM((clips, 2, rows // 2) + piece, jnp.bfloat16),
            pltpu.VMEM((clips, 2) + piece, jnp.bfloat16),
            pltpu.VMEM((clips, 2) + piece, jnp.bfloat16),
            pltpu.VMEM((clips - 1, 2) + piece, jnp.bfloat16),
            pltpu.VMEM((clips - 1, 2) + piece, jnp.bfloat16),
            dma((clips, 2)),
            dma((clips, 2, 2)),
            dma((clips, 2, 2)),
            dma((clips - 1, 2)),
        ],
        compiler_params=pltpu.CompilerParams(
            collective_id=1, has_side_effects=True, vmem_limit_bytes=48 * 1024 * 1024
        ),
        name="gradients",
    )(lhs, rhs)
    return out.reshape(2 * part_rows, lanes)


def local(
    current,
    bank,
    request,
    frame_pick,
    shift_rows,
    shift_cols,
    hist_count,
    join_weight,
    conv_one,
    conv_two,
    grad_out,
):
    height, width, channels = (current.shape[1], current.shape[2], current.shape[3])
    warped = fetch(bank[0], request, frame_pick, shift_rows, shift_cols, hist_count)
    cells = height * width
    stacked = jnp.concatenate([current.reshape(1, cells, channels), warped], axis=0)
    join_blocks = join_weight.reshape(HIST + 1, channels, channels)
    joined = jnp.einsum(
        "kpc,kcd->pd", stacked, join_blocks, preferred_element_type=jnp.float32
    ).astype(jnp.bfloat16)
    act = jnp.maximum(joined, 0)
    act_patch = forward_patch(act.reshape(height, width, channels))
    conv1 = jnp.einsum("tpc,tcd->pd", act_patch, conv_one.reshape(9, channels, channels), preferred_element_type=jnp.float32)
    hidden = jnp.maximum(conv1, 0.0).astype(jnp.bfloat16)
    hidden_patch = forward_patch(hidden.reshape(height, width, channels))
    conv2 = jnp.einsum("tpc,tcd->pd", hidden_patch, conv_two.reshape(9, channels, channels), preferred_element_type=jnp.float32)
    encoded = (
        (joined.astype(jnp.float32) + conv2)
        .astype(jnp.bfloat16)
        .reshape(1, height, width, channels)
    )
    upstream = grad_out[0]
    flat_up = upstream.reshape(cells, channels)
    d_hidden = jnp.einsum(
        "tpc,tcd->pd", backward_patch(upstream), flipped(conv_two), preferred_element_type=jnp.float32
    )
    d_conv1 = jnp.where(conv1 > 0, d_hidden, 0.0).astype(jnp.bfloat16)
    d_act = jnp.einsum(
        "tpc,tcd->pd",
        backward_patch(d_conv1.reshape(height, width, channels)),
        flipped(conv_one),
        preferred_element_type=jnp.float32,
    )
    d_joined = (flat_up.astype(jnp.float32) + jnp.where(joined > 0, d_act, 0.0)).astype(
        jnp.bfloat16
    )
    weight_grads = gradients(
        ((stacked, d_joined), (act_patch, d_conv1), (hidden_patch, flat_up))
    )
    return (encoded, weight_grads)


def solution(mesh):
    placed = (
        P("clip", "row", "col", None),
        P("clip", None, "row", "col", None),
        P(),
        P(),
        P(),
        P(),
        P(),
        P(),
        P(),
        P(),
        P("clip", "row", "col", None),
    )
    return jax.shard_map(
        local,
        mesh=mesh,
        in_specs=placed,
        out_specs=(P("clip", "row", "col", None), P(("clip", "row"), "col")),
        check_vma=False,
    )
```

```python
import jax
import jax.numpy as jnp
from jax import lax
from jax.experimental import pallas as pl
from jax.experimental.pallas import tpu as pltpu
from jax.sharding import PartitionSpec as P

HIST = 15


def fetch_kernel(
    served, wanted, bank, out, own, rim, chosen, got, near_sem, row_sem, col_sem, clip_sem, local_sem
):
    frames = bank.shape[0]
    clips = lax.axis_size("clip")
    rows = lax.axis_size("row")
    cols = lax.axis_size("col")
    capacity = got.shape[1] // clips
    clip = lax.axis_index("clip")
    row = lax.axis_index("row")
    col = lax.axis_index("col")
    up, down, left, right = row > 0, row < rows - 1, col > 0, col < cols - 1

    def signal(**where):
        pl.semaphore_signal(
            pltpu.get_barrier_semaphore(), inc=1, device_id=where, device_id_type=pl.DeviceIdType.MESH
        )

    def remote(source, target, sems, where):
        return pltpu.make_async_remote_copy(
            src_ref=source,
            dst_ref=target,
            send_sem=sems.at[0],
            recv_sem=sems.at[1],
            device_id=where,
            device_id_type=pl.DeviceIdType.MESH,
        )

    centre = pltpu.make_async_copy(bank, own.at[0:frames, :, :, 1:3], local_sem)
    centre.start()
    partners = [lax.rem(clip + step, clips) for step in range(1, clips)]
    for partner in partners:
        signal(clip=partner)
    for there, axis, index in (
        (up, "row", row - 1),
        (down, "row", row + 1),
        (left, "col", col - 1),
        (right, "col", col + 1),
    ):
        pl.when(there)(lambda axis=axis, index=index: signal(**{axis: index}))
    peers = clips - 1
    for there in (up, down, left, right):
        peers = peers + there.astype(jnp.int32)
    pl.semaphore_wait(pltpu.get_barrier_semaphore(), peers)

    to_right = remote(bank.at[:, :, :, 1], own.at[0:frames, :, :, 0], near_sem.at[0], {"col": col + 1})
    to_left = remote(bank.at[:, :, :, 0], own.at[0:frames, :, :, 3], near_sem.at[1], {"col": col - 1})
    to_down = remote(bank.at[:, 1], rim.at[0:frames, 0, :, 1:3], row_sem.at[0], {"row": row + 1})
    to_up = remote(bank.at[:, 0], rim.at[0:frames, 2, :, 1:3], row_sem.at[1], {"row": row - 1})
    pl.when(right)(to_right.start)
    pl.when(left)(to_left.start)
    pl.when(down)(to_down.start)
    pl.when(up)(to_up.start)

    own[frames] = jnp.zeros_like(own[frames])
    rim[frames] = jnp.zeros_like(rim[frames])

    def clear(view, place):
        for frame in range(frames):
            view[(frame,) + place] = jnp.zeros_like(view[(frame,) + place])

    every = slice(None)
    pl.when(jnp.logical_not(up))(lambda: clear(rim, (0,)))
    pl.when(jnp.logical_not(down))(lambda: clear(rim, (2,)))

    @pl.when(jnp.logical_not(left))
    def _():
        clear(own, (every, every, 0))
        clear(rim, (0, every, 0))
        clear(rim, (2, every, 0))

    @pl.when(jnp.logical_not(right))
    def _():
        clear(own, (every, every, 3))
        clear(rim, (0, every, 3))
        clear(rim, (2, every, 3))

    centre.wait()
    pl.when(left)(to_right.wait_recv)
    pl.when(right)(to_left.wait_recv)

    def decode(slot):
        packed = served[slot]
        shift_col = lax.rem(packed, 3) - 1
        rest = lax.div(packed, 3)
        return lax.div(rest, 3), lax.rem(rest, 3) - 1, shift_col

    def pick(part, target, partner):
        for spot in range(capacity):
            slot = partner * capacity + spot
            frame, shift_row, shift_col = decode(slot)
            if part == 0:
                line = jnp.where(shift_row < 0, 1, 0)
                target[0, slot] = own[frame, line, :, pl.ds(1 - shift_col, 2)]
            else:
                target[1, slot] = rim[frame, 1 - shift_row, :, pl.ds(1 - shift_col, 2)]

    sends = []

    def send(part, step):
        copy = remote(
            chosen.at[part, pl.ds(partners[step - 1] * capacity, capacity)],
            got.at[part, pl.ds(clip * capacity, capacity)],
            clip_sem.at[part, step - 1],
            {"clip": partners[step - 1]},
        )
        copy.start()
        sends.append(copy)

    for part in range(2):
        if part == 1:
            def keep(frame, carry):
                rim[frame, 1] = own[frame, 1]
                return carry

            lax.fori_loop(0, frames, keep, 0)
            pl.when(up)(to_down.wait_recv)
            pl.when(down)(to_up.wait_recv)
            corners = [
                (up, right, remote(rim.at[0:frames, 0, :, 2], rim.at[0:frames, 0, :, 0], col_sem.at[0], {"col": col + 1})),
                (down, right, remote(rim.at[0:frames, 2, :, 2], rim.at[0:frames, 2, :, 0], col_sem.at[1], {"col": col + 1})),
                (up, left, remote(rim.at[0:frames, 0, :, 1], rim.at[0:frames, 0, :, 3], col_sem.at[2], {"col": col - 1})),
                (down, left, remote(rim.at[0:frames, 2, :, 1], rim.at[0:frames, 2, :, 3], col_sem.at[3], {"col": col - 1})),
            ]
            for vertical, side, copy in corners:
                pl.when(jnp.logical_and(vertical, side))(copy.start)
            for (vertical, _, copy), other in zip(corners, (left, left, right, right)):
                pl.when(jnp.logical_and(vertical, other))(copy.wait_recv)
        for step in range(1, clips):
            pick(part, chosen, partners[step - 1])
            if step > 1:
                send(part, step - 1)
        pick(part, got, clip)
        send(part, clips - 1)
    for copy in sends:
        copy.wait_recv()
    slots = out.shape[0]
    for slot in range(slots):
        packed = wanted[slot]
        place = lax.div(packed, 2)
        flag = lax.rem(packed, 2)
        out[slot, 0] = got[flag, place]
        out[slot, 1] = got[1 - flag, place]
    for copy in sends:
        copy.wait_send()
    pl.when(right)(to_right.wait_send)
    pl.when(left)(to_left.wait_send)
    pl.when(down)(to_down.wait_send)
    pl.when(up)(to_up.wait_send)
    for vertical, side, copy in corners:
        pl.when(jnp.logical_and(vertical, side))(copy.wait_send)


def fetch(bank, request, frame_pick, shift_rows, shift_cols, hist_count):
    frames, height, width, channels = bank.shape
    clips = lax.axis_size("clip")
    capacity = (HIST + clips - 1) // clips
    own_clip = lax.axis_index("clip")
    slot_ids = own_clip * capacity + jnp.arange(capacity, dtype=jnp.int32)
    matches = (request[:, None, :] == slot_ids[None, :, None]).astype(jnp.int32)
    valid = jnp.arange(HIST)[None, :] < hist_count[:, None]
    frame = jnp.where(valid, frame_pick, frames)
    packed = (frame * 3 + shift_rows + 1) * 3 + shift_cols + 1
    served = jnp.sum(matches * packed[:, None, :], axis=-1).reshape(-1)
    pair = request * 2 + (shift_rows == 1).astype(jnp.int32)
    wanted = lax.dynamic_index_in_dim(pair, own_clip, 0, False)
    half = (height // 2, 2, width // 2, channels)
    blocks = bank.reshape((frames, 2) + half)
    wide = (height // 2, 4, width // 2, channels)
    smem = pl.BlockSpec(memory_space=pltpu.SMEM)
    dma = pltpu.SemaphoreType.DMA
    out = pl.pallas_call(
        fetch_kernel,
        out_shape=jax.ShapeDtypeStruct((HIST, 2) + half, bank.dtype),
        in_specs=[smem, smem, pl.BlockSpec(memory_space=pl.ANY)],
        out_specs=pl.BlockSpec(memory_space=pltpu.VMEM),
        scratch_shapes=[
            pltpu.VMEM((frames + 1, 2) + wide, bank.dtype),
            pltpu.VMEM((frames + 1, 3) + wide, bank.dtype),
            pltpu.VMEM((2, clips * capacity) + half, bank.dtype),
            pltpu.VMEM((2, clips * capacity) + half, bank.dtype),
            dma((2, 2)),
            dma((2, 2)),
            dma((4, 2)),
            dma((2, clips - 1, 2)),
            dma,
        ],
        compiler_params=pltpu.CompilerParams(
            collective_id=0, has_side_effects=True, vmem_limit_bytes=40 * 1024 * 1024
        ),
        name="fetch",
    )(served, wanted, blocks)
    return out.reshape(HIST, height * width, channels)


SIDES = [(down, right) for down in (-1, 0, 1) for right in (-1, 0, 1) if (down, right) != (0, 0)]


def block_kernel(
    joined, upstream, conv_one, conv_two, encoded, d_joined, act_views, hidden_views, d_conv1,
    up_views, back_views, field, conv1, edge, sent, came, sems
):
    rows, cols = lax.axis_size("row"), lax.axis_size("col")
    row, col = lax.axis_index("row"), lax.axis_index("col")
    height, width = act_views.shape[1] - 2, act_views.shape[2]
    cells, channels = joined.shape

    def there(down, right):
        first = jnp.logical_and(row + down >= 0, row + down < rows)
        return jnp.logical_and(first, jnp.logical_and(col + right >= 0, col + right < cols))

    peers = 0
    for down, right in SIDES:
        found = there(down, right)
        peers = peers + found.astype(jnp.int32)

        @pl.when(found)
        def _(down=down, right=right):
            pl.semaphore_signal(
                pltpu.get_barrier_semaphore(),
                inc=1,
                device_id={"row": row + down, "col": col + right},
                device_id_type=pl.DeviceIdType.MESH,
            )

    pl.semaphore_wait(pltpu.get_barrier_semaphore(), peers)
    for index, (down, right) in enumerate(SIDES):

        @pl.when(jnp.logical_not(there(-down, -right)))
        def _(index=index):
            for which in range(4):
                came[which, index] = jnp.zeros_like(came[which, index])

    def copies(which):
        made = []
        for index, (down, right) in enumerate(SIDES):
            source = {-1: 0, 1: 1}.get(down, 2 if right < 0 else 3)
            made.append(
                pltpu.make_async_remote_copy(
                    src_ref=sent.at[which, source],
                    dst_ref=came.at[which, index],
                    send_sem=sems.at[which, index, 0],
                    recv_sem=sems.at[which, index, 1],
                    device_id={"row": row + down, "col": col + right},
                    device_id_type=pl.DeviceIdType.MESH,
                )
            )
        return made

    def line(which, place):
        return field[which, place * width : (place + 1) * width, :]

    def begin(which, value):
        field[which] = value
        sent[which, 0] = line(which, 0).astype(sent.dtype)
        sent[which, 1] = line(which, height - 1).astype(sent.dtype)
        for place in range(height):
            here = line(which, place)
            edge[0, place : place + 1, :] = here[0:1]
            edge[1, place : place + 1, :] = here[width - 1 : width]
        sent[which, 2] = edge[0].astype(sent.dtype)
        sent[which, 3] = edge[1].astype(sent.dtype)
        for copy, side in zip(copies(which), SIDES):
            pl.when(there(*side))(copy.start)

    def finish(which, views):
        for copy, (down, right) in zip(copies(which), SIDES):
            pl.when(there(-down, -right))(copy.wait_recv)

        def got(down, right):
            return came[which, SIDES.index((down, right))].astype(jnp.float32)

        lefts, rights = got(0, 1), got(0, -1)
        for place in range(height + 2):
            if place == 0 or place == height + 1:
                sign = 1 if place == 0 else -1
                here = got(sign, 0)
                before = got(sign, 1)[width - 1 : width]
                after = got(sign, -1)[0:1]
            else:
                here = line(which, place - 1)
                before = lefts[place - 1 : place]
                after = rights[place - 1 : place]
            views[0, place] = jnp.concatenate([before, here[: width - 1]], axis=0).astype(views.dtype)
            views[1, place] = here.astype(views.dtype)
            views[2, place] = jnp.concatenate([here[1:], after], axis=0).astype(views.dtype)

    def convolve(views, weight, mirror):
        total = None
        for tap in range(9):
            top, left = tap // 3, tap % 3
            if mirror:
                top, left = 2 - top, 2 - left
            view = views[left, top : top + height].reshape(cells, channels)
            block = weight[tap * channels : (tap + 1) * channels, :]
            term = lax.dot_general(
                view, block, (((1,), (1 if mirror else 0,)), ((), ())), preferred_element_type=jnp.float32
            )
            total = term if total is None else total + term
        return total

    begin(0, jnp.maximum(joined[...].astype(jnp.float32), 0.0))
    begin(1, upstream[...].astype(jnp.float32))
    finish(0, act_views)
    conv1[...] = convolve(act_views, conv_one, False)
    begin(2, jnp.maximum(conv1[...], 0.0).astype(jnp.bfloat16).astype(jnp.float32))
    finish(1, up_views)
    masked = jnp.where(conv1[...] > 0.0, convolve(up_views, conv_two, True), 0.0).astype(jnp.bfloat16)
    d_conv1[...] = masked
    begin(3, masked.astype(jnp.float32))
    finish(2, hidden_views)
    encoded[...] = (joined[...].astype(jnp.float32) + convolve(hidden_views, conv_two, False)).astype(
        jnp.bfloat16
    )
    finish(3, back_views)
    d_act = convolve(back_views, conv_one, True)
    d_joined[...] = (
        upstream[...].astype(jnp.float32) + jnp.where(joined[...].astype(jnp.float32) > 0.0, d_act, 0.0)
    ).astype(jnp.bfloat16)
    for which in range(4):
        for copy, side in zip(copies(which), SIDES):
            pl.when(there(*side))(copy.wait_send)


def residual_block(joined, upstream, conv_one, conv_two, height, width):
    cells, channels = joined.shape
    flat = jax.ShapeDtypeStruct((cells, channels), jnp.bfloat16)
    views = jax.ShapeDtypeStruct((3, height + 2, width, channels), jnp.bfloat16)
    vmem = pl.BlockSpec(memory_space=pltpu.VMEM)
    return pl.pallas_call(
        block_kernel,
        out_shape=(flat, flat, views, views, flat),
        in_specs=[vmem] * 4,
        out_specs=(vmem,) * 5,
        scratch_shapes=[
            pltpu.VMEM(views.shape, jnp.bfloat16),
            pltpu.VMEM(views.shape, jnp.bfloat16),
            pltpu.VMEM((4, cells, channels), jnp.float32),
            pltpu.VMEM((cells, channels), jnp.float32),
            pltpu.VMEM((2, height, channels), jnp.float32),
            pltpu.VMEM((4, 4, width, channels), jnp.bfloat16),
            pltpu.VMEM((4, 8, width, channels), jnp.bfloat16),
            pltpu.SemaphoreType.DMA((4, 8, 2)),
        ],
        compiler_params=pltpu.CompilerParams(
            collective_id=2, has_side_effects=True, vmem_limit_bytes=40 * 1024 * 1024
        ),
        name="block",
    )(joined, upstream, conv_one, conv_two)


def flip(index, bit):
    return index + bit - 2 * bit * lax.rem(lax.div(index, bit), 2)


def gradient_kernel(
    stacked, act_views, hidden_views, d_joined, d_conv1, upstream, out, term, near_out, near_in, far_out, far_in, last_out, last_in, clip_out, clip_in,
    near_sem, far_sem, last_sem, clip_sem
):
    clips = lax.axis_size("clip")
    rows = lax.axis_size("row")
    clip = lax.axis_index("clip")
    row = lax.axis_index("row")
    col = lax.axis_index("col")
    bits = (1, 2)
    peers = [{"col": 1 - col}] + [{"row": flip(row, bit)} for bit in bits]
    peers += [{"clip": lax.rem(clip + step, clips)} for step in range(1, clips)]
    for where in peers:
        pl.semaphore_signal(
            pltpu.get_barrier_semaphore(), inc=1, device_id=where, device_id_type=pl.DeviceIdType.MESH
        )
    pl.semaphore_wait(pltpu.get_barrier_semaphore(), len(peers))

    def remote(source, target, sems, where):
        return pltpu.make_async_remote_copy(
            src_ref=source,
            dst_ref=target,
            send_sem=sems.at[0],
            recv_sem=sems.at[1],
            device_id=where,
            device_id_type=pl.DeviceIdType.MESH,
        )

    size = stacked.shape[2]
    lanes = term.shape[4]
    part_rows = term.shape[3]
    height = act_views.shape[1] - 2
    index = 0
    for group, (count, right) in enumerate(((stacked.shape[0], d_joined), (9, d_conv1), (9, upstream))):
        for spot in range(count):
            if group == 0:
                left = stacked[spot]
            else:
                views = act_views if group == 1 else hidden_views
                left = views[spot % 3, spot // 3 : spot // 3 + height].reshape(right.shape)
            product = lax.dot_general(
                left, right[...], (((0,), (0,)), ((), ())), preferred_element_type=jnp.float32
            )
            start = index * size
            done = 0
            while done < size:
                place = start + done
                piece = place // part_rows
                inside = place % part_rows
                length = min(size - done, part_rows - inside)
                for side in range(2):
                    term[side, piece // 2, piece % 2, inside : inside + length] = product[
                        done : done + length, side * lanes : (side + 1) * lanes
                    ]
                done += length
            index += 1

    order = [lax.rem(clip + step, clips) for step in range(1, clips)] + [clip]
    near = []
    for turn, target in enumerate(order):
        for spot in range(rows):
            block = target * rows + spot
            near_out[block] = term[1 - col, block].astype(near_out.dtype)
        near.append(
            remote(
                near_out.at[pl.ds(target * rows, rows)],
                near_in.at[pl.ds(target * rows, rows)],
                near_sem.at[turn],
                {"col": 1 - col},
            )
        )
        near[-1].start()

    def near_sum(turn, part, offset):
        spot = row
        for bit in bits:
            if offset & bit:
                spot = flip(spot, bit)
        block = order[turn] * rows + spot
        return term[col, block, part] + near_in[block, part].astype(jnp.float32)

    far, last, final = {}, {}, []

    def first(turn):
        near[turn].wait_recv()
        for part in range(2):
            one, two = bits if part == 0 else bits[::-1]
            for spot, offset in enumerate((one, one + two)):
                far_out[turn, part, spot] = near_sum(turn, part, offset).astype(far_out.dtype)
            far[turn, part] = remote(
                far_out.at[turn, part], far_in.at[turn, part], far_sem.at[turn, part], {"row": flip(row, one)}
            )
            far[turn, part].start()

    def second(turn):
        for part in range(2):
            one, two = bits if part == 0 else bits[::-1]
            far[turn, part].wait_recv()
            total = near_sum(turn, part, two) + far_in[turn, part, 1].astype(jnp.float32)
            last_out[turn, part] = total.astype(last_out.dtype)
            last[turn, part] = remote(
                last_out.at[turn, part], last_in.at[turn, part], last_sem.at[turn, part], {"row": flip(row, two)}
            )
            last[turn, part].start()

    def third(turn):
        for part in range(2):
            last[turn, part].wait_recv()
            total = near_sum(turn, part, 0) + far_in[turn, part, 0].astype(jnp.float32)
            total = total + last_in[turn, part].astype(jnp.float32)
            if turn < clips - 1:
                clip_out[turn, part] = total.astype(clip_out.dtype)
            else:
                out[part] = total
        if turn < clips - 1:
            copy = remote(clip_out.at[turn], clip_in.at[turn], clip_sem.at[turn], {"clip": order[turn]})
            copy.start()
            final.append(copy)

    for turn in range(clips + 2):
        if turn < clips:
            first(turn)
        if 0 <= turn - 1 < clips:
            second(turn - 1)
        if turn >= 2:
            third(turn - 2)
    for turn, copy in enumerate(final):
        copy.wait_recv()
        for part in range(2):
            out[part] += clip_in[turn, part].astype(jnp.float32)
    for copy in near + list(far.values()) + list(last.values()) + final:
        copy.wait_send()


def gradients(*operands):
    stacked = operands[0]
    clips = lax.axis_size("clip")
    rows = lax.axis_size("row")
    total = (stacked.shape[0] + 18) * stacked.shape[2]
    part_rows = total // (2 * clips * rows)
    lanes = stacked.shape[2] // lax.axis_size("col")
    piece = (part_rows, lanes)
    vmem = pl.BlockSpec(memory_space=pltpu.VMEM)
    dma = pltpu.SemaphoreType.DMA
    out = pl.pallas_call(
        gradient_kernel,
        out_shape=jax.ShapeDtypeStruct((2,) + piece, jnp.float32),
        in_specs=[vmem] * 6,
        out_specs=vmem,
        scratch_shapes=[
            pltpu.VMEM((2, clips * rows, 2) + piece, jnp.float32),
            pltpu.VMEM((clips * rows, 2) + piece, jnp.bfloat16),
            pltpu.VMEM((clips * rows, 2) + piece, jnp.bfloat16),
            pltpu.VMEM((clips, 2, rows // 2) + piece, jnp.bfloat16),
            pltpu.VMEM((clips, 2, rows // 2) + piece, jnp.bfloat16),
            pltpu.VMEM((clips, 2) + piece, jnp.bfloat16),
            pltpu.VMEM((clips, 2) + piece, jnp.bfloat16),
            pltpu.VMEM((clips - 1, 2) + piece, jnp.bfloat16),
            pltpu.VMEM((clips - 1, 2) + piece, jnp.bfloat16),
            dma((clips, 2)),
            dma((clips, 2, 2)),
            dma((clips, 2, 2)),
            dma((clips - 1, 2)),
        ],
        compiler_params=pltpu.CompilerParams(
            collective_id=1, has_side_effects=True, vmem_limit_bytes=48 * 1024 * 1024
        ),
        name="gradients",
    )(*operands)
    return out.reshape(2 * part_rows, lanes)


def local(
    current,
    bank,
    request,
    frame_pick,
    shift_rows,
    shift_cols,
    hist_count,
    join_weight,
    conv_one,
    conv_two,
    grad_out,
):
    height, width, channels = (current.shape[1], current.shape[2], current.shape[3])
    warped = fetch(bank[0], request, frame_pick, shift_rows, shift_cols, hist_count)
    cells = height * width
    stacked = jnp.concatenate([current.reshape(1, cells, channels), warped], axis=0)
    join_blocks = join_weight.reshape(HIST + 1, channels, channels)
    joined = jnp.einsum(
        "kpc,kcd->pd", stacked, join_blocks, preferred_element_type=jnp.float32
    ).astype(jnp.bfloat16)
    upstream = grad_out.reshape(cells, channels)
    encoded, d_joined, act_views, hidden_views, d_conv1 = residual_block(
        joined, upstream, conv_one, conv_two, height, width
    )
    encoded = encoded.reshape(1, height, width, channels)
    weight_grads = gradients(stacked, act_views, hidden_views, d_joined, d_conv1, upstream)
    return (encoded, weight_grads)


def solution(mesh):
    placed = (
        P("clip", "row", "col", None),
        P("clip", None, "row", "col", None),
        P(),
        P(),
        P(),
        P(),
        P(),
        P(),
        P(),
        P(),
        P("clip", "row", "col", None),
    )
    return jax.shard_map(
        local,
        mesh=mesh,
        in_specs=placed,
        out_specs=(P("clip", "row", "col", None), P(("clip", "row"), "col")),
        check_vma=False,
    )
```

```python
import jax
import jax.numpy as jnp
from jax import lax
from jax.experimental import pallas as pl
from jax.experimental.pallas import tpu as pltpu
from jax.sharding import PartitionSpec as P

HIST = 15


def fetch_kernel(
    request, picks, shift_rows, shift_cols, counts, bank, out, table, core, own, rim, chosen, got,
    near_sem, row_sem, col_sem, clip_sem, local_sem
):
    frames = bank.shape[0]
    clips = lax.axis_size("clip")
    rows = lax.axis_size("row")
    cols = lax.axis_size("col")
    capacity = got.shape[1] // clips
    clip = lax.axis_index("clip")
    row = lax.axis_index("row")
    col = lax.axis_index("col")
    up, down, left, right = row > 0, row < rows - 1, col > 0, col < cols - 1

    def signal(**where):
        pl.semaphore_signal(
            pltpu.get_barrier_semaphore(), inc=1, device_id=where, device_id_type=pl.DeviceIdType.MESH
        )

    def remote(source, target, sems, where):
        return pltpu.make_async_remote_copy(
            src_ref=source,
            dst_ref=target,
            send_sem=sems.at[0],
            recv_sem=sems.at[1],
            device_id=where,
            device_id_type=pl.DeviceIdType.MESH,
        )

    inner = pltpu.make_async_copy(bank, core.at[0:frames], local_sem.at[0])
    inner.start()
    centre = pltpu.make_async_copy(bank, own.at[0:frames, :, :, 1:3], local_sem.at[1])
    centre.start()
    partners = [lax.rem(clip + step, clips) for step in range(1, clips)]
    for partner in partners:
        signal(clip=partner)
    for there, axis, index in (
        (up, "row", row - 1),
        (down, "row", row + 1),
        (left, "col", col - 1),
        (right, "col", col + 1),
    ):
        pl.when(there)(lambda axis=axis, index=index: signal(**{axis: index}))
    peers = clips - 1
    for there in (up, down, left, right):
        peers = peers + there.astype(jnp.int32)
    pl.semaphore_wait(pltpu.get_barrier_semaphore(), peers)

    to_right = remote(bank.at[:, :, :, 1], own.at[0:frames, :, :, 0], near_sem.at[0], {"col": col + 1})
    to_left = remote(bank.at[:, :, :, 0], own.at[0:frames, :, :, 3], near_sem.at[1], {"col": col - 1})
    to_down = remote(bank.at[:, 1], rim.at[0:frames, 0, :, 1:3], row_sem.at[0], {"row": row + 1})
    to_up = remote(bank.at[:, 0], rim.at[0:frames, 2, :, 1:3], row_sem.at[1], {"row": row - 1})
    pl.when(right)(to_right.start)
    pl.when(left)(to_left.start)
    pl.when(down)(to_down.start)
    pl.when(up)(to_up.start)

    core[frames] = jnp.zeros_like(core[frames])

    def match(slot, carry):
        partner = lax.div(slot, capacity)
        target = clip * capacity + lax.rem(slot, capacity)
        found = jnp.int32(0)
        for spot in range(out.shape[0]):
            frame = jnp.where(spot < counts[partner], picks[partner, spot], frames)
            packed = (frame * 3 + shift_rows[partner, spot] + 1) * 3 + shift_cols[partner, spot] + 1
            found = jnp.where(request[partner, spot] == target, packed, found)
        table[slot] = found
        return carry

    lax.fori_loop(0, clips * capacity, match, 0)

    def decode(slot):
        packed = table[slot]
        shift_col = lax.rem(packed, 3) - 1
        rest = lax.div(packed, 3)
        return lax.div(rest, 3), lax.rem(rest, 3) - 1, shift_col

    def pick(part, target, partner):
        for spot in range(capacity):
            slot = partner * capacity + spot
            frame, shift_row, shift_col = decode(slot)
            line = jnp.where(shift_row < 0, 1, 0)
            near = jnp.where(shift_col < 0, 1, 0)
            away = jnp.where(shift_col == 0, 2, jnp.where(shift_col > 0, 0, 3))
            if part == 0:
                target[0, slot] = core[frame, line, :, near]
            elif part == 1:
                target[1, slot] = own[frame, line, :, away]
            else:
                target[part, slot] = rim[frame, 1 - shift_row, :, near + 1 if part == 2 else away]

    sends = []

    def send(part, step):
        copy = remote(
            chosen.at[part, pl.ds(partners[step - 1] * capacity, capacity)],
            got.at[part, pl.ds(clip * capacity, capacity)],
            clip_sem.at[part, step - 1],
            {"clip": partners[step - 1]},
        )
        copy.start()
        sends.append(copy)

    def serve(part):
        for step in range(1, clips):
            pick(part, chosen, partners[step - 1])
            if step > 1:
                send(part, step - 1)
        pick(part, got, clip)
        send(part, clips - 1)

    inner.wait()
    serve(0)
    own[frames] = jnp.zeros_like(own[frames])
    rim[frames] = jnp.zeros_like(rim[frames])

    def clear(view, place):
        for frame in range(frames):
            view[(frame,) + place] = jnp.zeros_like(view[(frame,) + place])

    every = slice(None)
    pl.when(jnp.logical_not(up))(lambda: clear(rim, (0,)))
    pl.when(jnp.logical_not(down))(lambda: clear(rim, (2,)))

    @pl.when(jnp.logical_not(left))
    def _():
        clear(own, (every, every, 0))
        clear(rim, (0, every, 0))
        clear(rim, (2, every, 0))

    @pl.when(jnp.logical_not(right))
    def _():
        clear(own, (every, every, 3))
        clear(rim, (0, every, 3))
        clear(rim, (2, every, 3))

    centre.wait()
    pl.when(left)(to_right.wait_recv)
    pl.when(right)(to_left.wait_recv)

    for part in range(1, 4):
        if part == 2:
            def keep(frame, carry):
                rim[frame, 1] = own[frame, 1]
                return carry

            lax.fori_loop(0, frames, keep, 0)
            pl.when(up)(to_down.wait_recv)
            pl.when(down)(to_up.wait_recv)
            corners = [
                (up, right, remote(rim.at[0:frames, 0, :, 2], rim.at[0:frames, 0, :, 0], col_sem.at[0], {"col": col + 1})),
                (down, right, remote(rim.at[0:frames, 2, :, 2], rim.at[0:frames, 2, :, 0], col_sem.at[1], {"col": col + 1})),
                (up, left, remote(rim.at[0:frames, 0, :, 1], rim.at[0:frames, 0, :, 3], col_sem.at[2], {"col": col - 1})),
                (down, left, remote(rim.at[0:frames, 2, :, 1], rim.at[0:frames, 2, :, 3], col_sem.at[3], {"col": col - 1})),
            ]
            for vertical, side, copy in corners:
                pl.when(jnp.logical_and(vertical, side))(copy.start)
            for (vertical, _, copy), other in zip(corners, (left, left, right, right)):
                pl.when(jnp.logical_and(vertical, other))(copy.wait_recv)
        serve(part)
    for copy in sends:
        copy.wait_recv()
    slots = out.shape[0]
    for slot in range(slots):
        place = request[clip, slot]
        below = jnp.where(shift_rows[clip, slot] > 0, 1, 0)
        beside = jnp.where(shift_cols[clip, slot] > 0, 1, 0)
        for line in range(2):
            for lane in range(2):
                first = 1 - below if line else below
                second = 1 - beside if lane else beside
                out[slot, line, :, lane] = got[2 * first + second, place]
    for copy in sends:
        copy.wait_send()
    pl.when(right)(to_right.wait_send)
    pl.when(left)(to_left.wait_send)
    pl.when(down)(to_down.wait_send)
    pl.when(up)(to_up.wait_send)
    for vertical, side, copy in corners:
        pl.when(jnp.logical_and(vertical, side))(copy.wait_send)


def fetch(bank, request, frame_pick, shift_rows, shift_cols, hist_count):
    frames, height, width, channels = bank.shape
    clips = lax.axis_size("clip")
    capacity = (HIST + clips - 1) // clips
    half = (height // 2, 2, width // 2, channels)
    blocks = bank.reshape((frames, 2) + half)
    wide = (height // 2, 4, width // 2, channels)
    smem = pl.BlockSpec(memory_space=pltpu.SMEM)
    dma = pltpu.SemaphoreType.DMA
    out = pl.pallas_call(
        fetch_kernel,
        out_shape=jax.ShapeDtypeStruct((HIST, 2) + half, bank.dtype),
        in_specs=[smem] * 5 + [pl.BlockSpec(memory_space=pl.ANY)],
        out_specs=pl.BlockSpec(memory_space=pltpu.VMEM),
        scratch_shapes=[
            pltpu.SMEM((clips * capacity,), jnp.int32),
            pltpu.VMEM((frames + 1, 2) + half, bank.dtype),
            pltpu.VMEM((frames + 1, 2) + wide, bank.dtype),
            pltpu.VMEM((frames + 1, 3) + wide, bank.dtype),
            pltpu.VMEM((4, clips * capacity, height // 2, width // 2, channels), bank.dtype),
            pltpu.VMEM((4, clips * capacity, height // 2, width // 2, channels), bank.dtype),
            dma((2, 2)),
            dma((2, 2)),
            dma((4, 2)),
            dma((4, clips - 1, 2)),
            dma((2,)),
        ],
        compiler_params=pltpu.CompilerParams(
            collective_id=0, has_side_effects=True, vmem_limit_bytes=40 * 1024 * 1024
        ),
        name="fetch",
    )(request, frame_pick, shift_rows, shift_cols, hist_count, blocks)
    return out.reshape(HIST, height * width, channels)


SIDES = [(down, right) for down in (-1, 0, 1) for right in (-1, 0, 1) if (down, right) != (0, 0)]


def block_kernel(
    joined, upstream, conv_one, conv_two, encoded, d_joined, act_views, hidden_views, d_conv1,
    up_views, back_views, field, conv1, edge, sent, came, sems
):
    rows, cols = lax.axis_size("row"), lax.axis_size("col")
    row, col = lax.axis_index("row"), lax.axis_index("col")
    height, width = act_views.shape[1] - 2, act_views.shape[2]
    cells, channels = joined.shape

    def there(down, right):
        first = jnp.logical_and(row + down >= 0, row + down < rows)
        return jnp.logical_and(first, jnp.logical_and(col + right >= 0, col + right < cols))

    peers = 0
    for down, right in SIDES:
        found = there(down, right)
        peers = peers + found.astype(jnp.int32)

        @pl.when(found)
        def _(down=down, right=right):
            pl.semaphore_signal(
                pltpu.get_barrier_semaphore(),
                inc=1,
                device_id={"row": row + down, "col": col + right},
                device_id_type=pl.DeviceIdType.MESH,
            )

    pl.semaphore_wait(pltpu.get_barrier_semaphore(), peers)
    for index, (down, right) in enumerate(SIDES):

        @pl.when(jnp.logical_not(there(-down, -right)))
        def _(index=index):
            for which in range(4):
                came[which, index] = jnp.zeros_like(came[which, index])

    def copies(which):
        made = []
        for index, (down, right) in enumerate(SIDES):
            source = {-1: 0, 1: 1}.get(down, 2 if right < 0 else 3)
            made.append(
                pltpu.make_async_remote_copy(
                    src_ref=sent.at[which, source],
                    dst_ref=came.at[which, index],
                    send_sem=sems.at[which, index, 0],
                    recv_sem=sems.at[which, index, 1],
                    device_id={"row": row + down, "col": col + right},
                    device_id_type=pl.DeviceIdType.MESH,
                )
            )
        return made

    def line(which, place):
        return field[which, place * width : (place + 1) * width, :]

    def begin(which, value):
        field[which] = value
        sent[which, 0] = line(which, 0).astype(sent.dtype)
        sent[which, 1] = line(which, height - 1).astype(sent.dtype)
        for place in range(height):
            here = line(which, place)
            edge[0, place : place + 1, :] = here[0:1]
            edge[1, place : place + 1, :] = here[width - 1 : width]
        sent[which, 2] = edge[0].astype(sent.dtype)
        sent[which, 3] = edge[1].astype(sent.dtype)
        for copy, side in zip(copies(which), SIDES):
            pl.when(there(*side))(copy.start)

    def finish(which, views):
        for copy, (down, right) in zip(copies(which), SIDES):
            pl.when(there(-down, -right))(copy.wait_recv)

        def got(down, right):
            return came[which, SIDES.index((down, right))].astype(jnp.float32)

        lefts, rights = got(0, 1), got(0, -1)
        for place in range(height + 2):
            if place == 0 or place == height + 1:
                sign = 1 if place == 0 else -1
                here = got(sign, 0)
                before = got(sign, 1)[width - 1 : width]
                after = got(sign, -1)[0:1]
            else:
                here = line(which, place - 1)
                before = lefts[place - 1 : place]
                after = rights[place - 1 : place]
            views[0, place] = jnp.concatenate([before, here[: width - 1]], axis=0).astype(views.dtype)
            views[1, place] = here.astype(views.dtype)
            views[2, place] = jnp.concatenate([here[1:], after], axis=0).astype(views.dtype)

    def convolve(views, weight, mirror):
        total = None
        for tap in range(9):
            top, left = tap // 3, tap % 3
            if mirror:
                top, left = 2 - top, 2 - left
            view = views[left, top : top + height].reshape(cells, channels)
            block = weight[tap * channels : (tap + 1) * channels, :]
            term = lax.dot_general(
                view, block, (((1,), (1 if mirror else 0,)), ((), ())), preferred_element_type=jnp.float32
            )
            total = term if total is None else total + term
        return total

    begin(0, jnp.maximum(joined[...].astype(jnp.float32), 0.0))
    begin(1, upstream[...].astype(jnp.float32))
    finish(0, act_views)
    conv1[...] = convolve(act_views, conv_one, False)
    begin(2, jnp.maximum(conv1[...], 0.0).astype(jnp.bfloat16).astype(jnp.float32))
    finish(1, up_views)
    masked = jnp.where(conv1[...] > 0.0, convolve(up_views, conv_two, True), 0.0).astype(jnp.bfloat16)
    d_conv1[...] = masked
    begin(3, masked.astype(jnp.float32))
    finish(2, hidden_views)
    encoded[...] = (joined[...].astype(jnp.float32) + convolve(hidden_views, conv_two, False)).astype(
        jnp.bfloat16
    )
    finish(3, back_views)
    d_act = convolve(back_views, conv_one, True)
    d_joined[...] = (
        upstream[...].astype(jnp.float32) + jnp.where(joined[...].astype(jnp.float32) > 0.0, d_act, 0.0)
    ).astype(jnp.bfloat16)
    for which in range(4):
        for copy, side in zip(copies(which), SIDES):
            pl.when(there(*side))(copy.wait_send)


def residual_block(joined, upstream, conv_one, conv_two, height, width):
    cells, channels = joined.shape
    flat = jax.ShapeDtypeStruct((cells, channels), jnp.bfloat16)
    views = jax.ShapeDtypeStruct((3, height + 2, width, channels), jnp.bfloat16)
    vmem = pl.BlockSpec(memory_space=pltpu.VMEM)
    return pl.pallas_call(
        block_kernel,
        out_shape=(flat, flat, views, views, flat),
        in_specs=[vmem] * 4,
        out_specs=(vmem,) * 5,
        scratch_shapes=[
            pltpu.VMEM(views.shape, jnp.bfloat16),
            pltpu.VMEM(views.shape, jnp.bfloat16),
            pltpu.VMEM((4, cells, channels), jnp.float32),
            pltpu.VMEM((cells, channels), jnp.float32),
            pltpu.VMEM((2, height, channels), jnp.float32),
            pltpu.VMEM((4, 4, width, channels), jnp.bfloat16),
            pltpu.VMEM((4, 8, width, channels), jnp.bfloat16),
            pltpu.SemaphoreType.DMA((4, 8, 2)),
        ],
        compiler_params=pltpu.CompilerParams(
            collective_id=2, has_side_effects=True, vmem_limit_bytes=40 * 1024 * 1024
        ),
        name="block",
    )(joined, upstream, conv_one, conv_two)


def flip(index, bit):
    return index + bit - 2 * bit * lax.rem(lax.div(index, bit), 2)


def gradient_kernel(
    stacked, act_views, hidden_views, d_joined, d_conv1, upstream, out, term, near_out, near_in, far_out, far_in, last_out, last_in, clip_out, clip_in,
    near_sem, far_sem, last_sem, clip_sem
):
    clips = lax.axis_size("clip")
    rows = lax.axis_size("row")
    clip = lax.axis_index("clip")
    row = lax.axis_index("row")
    col = lax.axis_index("col")
    bits = (1, 2)
    peers = [{"col": 1 - col}] + [{"row": flip(row, bit)} for bit in bits]
    peers += [{"clip": lax.rem(clip + step, clips)} for step in range(1, clips)]
    for where in peers:
        pl.semaphore_signal(
            pltpu.get_barrier_semaphore(), inc=1, device_id=where, device_id_type=pl.DeviceIdType.MESH
        )
    pl.semaphore_wait(pltpu.get_barrier_semaphore(), len(peers))

    def remote(source, target, sems, where):
        return pltpu.make_async_remote_copy(
            src_ref=source,
            dst_ref=target,
            send_sem=sems.at[0],
            recv_sem=sems.at[1],
            device_id=where,
            device_id_type=pl.DeviceIdType.MESH,
        )

    size = stacked.shape[2]
    lanes = term.shape[4]
    part_rows = term.shape[3]
    height = act_views.shape[1] - 2
    index = 0
    for group, (count, right) in enumerate(((stacked.shape[0], d_joined), (9, d_conv1), (9, upstream))):
        for spot in range(count):
            if group == 0:
                left = stacked[spot]
            else:
                views = act_views if group == 1 else hidden_views
                left = views[spot % 3, spot // 3 : spot // 3 + height].reshape(right.shape)
            product = lax.dot_general(
                left, right[...], (((0,), (0,)), ((), ())), preferred_element_type=jnp.float32
            )
            start = index * size
            done = 0
            while done < size:
                place = start + done
                piece = place // part_rows
                inside = place % part_rows
                length = min(size - done, part_rows - inside)
                for side in range(2):
                    term[side, piece // 2, piece % 2, inside : inside + length] = product[
                        done : done + length, side * lanes : (side + 1) * lanes
                    ]
                done += length
            index += 1

    order = [lax.rem(clip + step, clips) for step in range(1, clips)] + [clip]
    near = []
    for turn, target in enumerate(order):
        for spot in range(rows):
            block = target * rows + spot
            near_out[block] = term[1 - col, block].astype(near_out.dtype)
        near.append(
            remote(
                near_out.at[pl.ds(target * rows, rows)],
                near_in.at[pl.ds(target * rows, rows)],
                near_sem.at[turn],
                {"col": 1 - col},
            )
        )
        near[-1].start()

    def near_sum(turn, part, offset):
        spot = row
        for bit in bits:
            if offset & bit:
                spot = flip(spot, bit)
        block = order[turn] * rows + spot
        return term[col, block, part] + near_in[block, part].astype(jnp.float32)

    far, last, final = {}, {}, []

    def first(turn):
        near[turn].wait_recv()
        for part in range(2):
            one, two = bits if part == 0 else bits[::-1]
            for spot, offset in enumerate((one, one + two)):
                far_out[turn, part, spot] = near_sum(turn, part, offset).astype(far_out.dtype)
            far[turn, part] = remote(
                far_out.at[turn, part], far_in.at[turn, part], far_sem.at[turn, part], {"row": flip(row, one)}
            )
            far[turn, part].start()

    def second(turn):
        for part in range(2):
            one, two = bits if part == 0 else bits[::-1]
            far[turn, part].wait_recv()
            total = near_sum(turn, part, two) + far_in[turn, part, 1].astype(jnp.float32)
            last_out[turn, part] = total.astype(last_out.dtype)
            last[turn, part] = remote(
                last_out.at[turn, part], last_in.at[turn, part], last_sem.at[turn, part], {"row": flip(row, two)}
            )
            last[turn, part].start()

    def third(turn):
        for part in range(2):
            last[turn, part].wait_recv()
            total = near_sum(turn, part, 0) + far_in[turn, part, 0].astype(jnp.float32)
            total = total + last_in[turn, part].astype(jnp.float32)
            if turn < clips - 1:
                clip_out[turn, part] = total.astype(clip_out.dtype)
            else:
                out[part] = total
        if turn < clips - 1:
            copy = remote(clip_out.at[turn], clip_in.at[turn], clip_sem.at[turn], {"clip": order[turn]})
            copy.start()
            final.append(copy)

    for turn in range(clips + 2):
        if turn < clips:
            first(turn)
        if 0 <= turn - 1 < clips:
            second(turn - 1)
        if turn >= 2:
            third(turn - 2)
    for turn, copy in enumerate(final):
        copy.wait_recv()
        for part in range(2):
            out[part] += clip_in[turn, part].astype(jnp.float32)
    for copy in near + list(far.values()) + list(last.values()) + final:
        copy.wait_send()


def gradients(*operands):
    stacked = operands[0]
    clips = lax.axis_size("clip")
    rows = lax.axis_size("row")
    total = (stacked.shape[0] + 18) * stacked.shape[2]
    part_rows = total // (2 * clips * rows)
    lanes = stacked.shape[2] // lax.axis_size("col")
    piece = (part_rows, lanes)
    vmem = pl.BlockSpec(memory_space=pltpu.VMEM)
    dma = pltpu.SemaphoreType.DMA
    out = pl.pallas_call(
        gradient_kernel,
        out_shape=jax.ShapeDtypeStruct((2,) + piece, jnp.float32),
        in_specs=[vmem] * 6,
        out_specs=vmem,
        scratch_shapes=[
            pltpu.VMEM((2, clips * rows, 2) + piece, jnp.float32),
            pltpu.VMEM((clips * rows, 2) + piece, jnp.bfloat16),
            pltpu.VMEM((clips * rows, 2) + piece, jnp.bfloat16),
            pltpu.VMEM((clips, 2, rows // 2) + piece, jnp.bfloat16),
            pltpu.VMEM((clips, 2, rows // 2) + piece, jnp.bfloat16),
            pltpu.VMEM((clips, 2) + piece, jnp.bfloat16),
            pltpu.VMEM((clips, 2) + piece, jnp.bfloat16),
            pltpu.VMEM((clips - 1, 2) + piece, jnp.bfloat16),
            pltpu.VMEM((clips - 1, 2) + piece, jnp.bfloat16),
            dma((clips, 2)),
            dma((clips, 2, 2)),
            dma((clips, 2, 2)),
            dma((clips - 1, 2)),
        ],
        compiler_params=pltpu.CompilerParams(
            collective_id=1, has_side_effects=True, vmem_limit_bytes=48 * 1024 * 1024
        ),
        name="gradients",
    )(*operands)
    return out.reshape(2 * part_rows, lanes)


def local(
    current,
    bank,
    request,
    frame_pick,
    shift_rows,
    shift_cols,
    hist_count,
    join_weight,
    conv_one,
    conv_two,
    grad_out,
):
    height, width, channels = (current.shape[1], current.shape[2], current.shape[3])
    warped = fetch(bank[0], request, frame_pick, shift_rows, shift_cols, hist_count)
    cells = height * width
    stacked = jnp.concatenate([current.reshape(1, cells, channels), warped], axis=0)
    join_blocks = join_weight.reshape(HIST + 1, channels, channels)
    joined = jnp.einsum(
        "kpc,kcd->pd", stacked, join_blocks, preferred_element_type=jnp.float32
    ).astype(jnp.bfloat16)
    upstream = grad_out.reshape(cells, channels)
    encoded, d_joined, act_views, hidden_views, d_conv1 = residual_block(
        joined, upstream, conv_one, conv_two, height, width
    )
    encoded = encoded.reshape(1, height, width, channels)
    weight_grads = gradients(stacked, act_views, hidden_views, d_joined, d_conv1, upstream)
    return (encoded, weight_grads)


def solution(mesh):
    placed = (
        P("clip", "row", "col", None),
        P("clip", None, "row", "col", None),
        P(),
        P(),
        P(),
        P(),
        P(),
        P(),
        P(),
        P(),
        P("clip", "row", "col", None),
    )
    return jax.shard_map(
        local,
        mesh=mesh,
        in_specs=placed,
        out_specs=(P("clip", "row", "col", None), P(("clip", "row"), "col")),
        check_vma=False,
    )
```
